32 devices in a mesh: row: 8 (over y, x, core), col: 4 (over z).
Axes of the slice: x: 2, y: 2, z: 4, core: 2. Of those that a mesh axis runs over, the one named last changes fastest.
Arguments:
- vectors: bfloat16 [4, 16384], P(None, ('row', 'col')), may hold values from -6 to 6
- tile_values: bfloat16 [8, 4, 32, 4096], P('row', 'col'), may hold values from -0.75 to 0.75
- tile_rows: int32 [8, 4, 32], P('row', 'col'), may hold values from 0 to 31, as said below
- tile_cols: int32 [8, 4, 32], P('row', 'col'), may hold values from 0 to 63
- tile_scale: int32 [8, 4, 32], P('row', 'col'), may hold values from 0 to 63
- tile_count: int32 [8, 4], P('row', 'col'), may hold values from 2 to 32, as said below
- scale_table: float32 [64], replicated, may hold values from 0.1 to 1.5
Outputs:
- product: float32 [4, 16384], P(None, ('row', 'col'))
The draws below stay inside these ranges and needn't reach their ends.
Inputs may be any that keep to these rules, and one draw needn't show every extreme that they name: Slots 0 to tile_count - 1 of a device hold its tiles, later slots are ignored; some device has all 32 slots live. On device (r, c), each slot t below min(8, 2) holds a diagonal block: tile_rows[r, c, t] = c * 8 + t; the other slots are uniform over the range.
All inputs are finite; a program needn't handle non-finite values.
Results may differ from the reference program's by a relative error of at most 0.0003.
Values may be sent and summed in bfloat16 or wider, within the bound.
A program may use at most 64 MiB of HBM per device.

```python
import math
import jax
import jax.numpy as jnp
from jax import lax

TILE = 64
NVEC = 4
NSCALE = 64
V = 512
TILES_DEV = 32
GRID_ROWS = 8
GRID_COLS = 4
NV = 16384
N_ROW = 8
N_COL = 4


def diagonal_slots():
    return min(V // TILE, TILES_DEV // 16)


def draw_tile_rows(key, part):
    diag_count = diagonal_slots()
    random_rows = jax.random.randint(jax.random.fold_in(key, 11), (GRID_ROWS, GRID_COLS, TILES_DEV), 0, GRID_COLS * V // TILE)
    col_place = jnp.arange(GRID_COLS, dtype=jnp.int32)[None, :, None]
    slot_place = jnp.arange(TILES_DEV, dtype=jnp.int32)[None, None, :]
    own_blocks = col_place * (V // TILE) + slot_place
    return jnp.where(slot_place < diag_count, own_blocks, random_rows).astype(jnp.int32)


def draw_tile_cols(key, part):
    diag_count = diagonal_slots()
    random_cols = jax.random.randint(jax.random.fold_in(key, 13), (GRID_ROWS, GRID_COLS, TILES_DEV), 0, GRID_ROWS * V // TILE)
    row_place = jnp.arange(GRID_ROWS, dtype=jnp.int32)[:, None, None]
    slot_place = jnp.arange(TILES_DEV, dtype=jnp.int32)[None, None, :]
    own_blocks = row_place * (V // TILE) + slot_place
    return jnp.where(slot_place < diag_count, own_blocks, random_cols).astype(jnp.int32)


def draw_tile_count(key, part):
    split_keys = jax.random.split(jax.random.fold_in(key, 7), 3)
    heavy_mask = jax.random.randint(split_keys[0], (GRID_ROWS, GRID_COLS), 0, 8) == 0
    light_load = jax.random.randint(split_keys[1], (GRID_ROWS, GRID_COLS), TILES_DEV // 16, TILES_DEV // 2 + 1)
    slot_counts = jnp.where(heavy_mask, TILES_DEV, light_load).reshape(-1)
    chosen_one = jax.random.randint(split_keys[2], (), 0, GRID_ROWS * GRID_COLS)
    slot_counts = slot_counts.at[chosen_one].set(TILES_DEV)
    return slot_counts.reshape(GRID_ROWS, GRID_COLS).astype(jnp.int32)


def touch_ends(result, rng, low, largest):
    dims = result.shape
    index_at = [jax.random.randint(jax.random.fold_in(rng, axis), (), 0, dims[axis]) for axis in range(len(dims))]
    result = result.at[tuple(index_at)].set(low)
    longest = dims.index(max(dims))
    index_at[longest] = (index_at[longest] + 1) % dims[longest]
    return result.at[tuple(index_at)].set(largest)


def shard_levels(stream_key, dims, cuts, smallest, top_value):
    def one(dim, shards_of):
        heights = jax.random.uniform(jax.random.fold_in(jax.random.fold_in(stream_key, 6), dim), (shards_of,), jnp.float32, smallest / len(cuts), top_value / len(cuts))
        return jnp.repeat(jnp.exp(heights), dims[dim] // shards_of).reshape((-1,) + (1,) * (len(dims) - dim - 1))

    loudness = one(*cuts[0])
    for cut in cuts[1:]:
        loudness = loudness * one(*cut)
    return loudness


def scatter_about(rng, shape, width, most, cuts=(), kind=jnp.bfloat16):
    array = jax.random.normal(rng, shape, jnp.float32) * width
    if len(cuts) > 0:
        array = shard_levels(rng, shape, cuts, -0.22, 0.18) * array
    return jnp.clip(array, min=-most, max=most).astype(kind)


def setup_inputs(seed: int = 0) -> dict:
    streams_of = jax.random.split(jax.random.key(seed), 8)
    vectors = scatter_about(streams_of[0], (NVEC, NV), 1.0, 6.0, ((1, 32),))
    tile_values = scatter_about(streams_of[1], (GRID_ROWS, GRID_COLS, TILES_DEV, TILE * TILE), TILE ** -0.5, 0.75, ((0, 8), (1, 4)))
    tile_rows = draw_tile_rows(jax.random.fold_in(streams_of[7], 71), 0)
    tile_cols = draw_tile_cols(jax.random.fold_in(streams_of[7], 71), 0)
    tile_scale = touch_ends(jax.random.randint(streams_of[4], (GRID_ROWS, GRID_COLS, TILES_DEV), 0, NSCALE), jax.random.fold_in(streams_of[4], 1), 0, NSCALE - 1).astype(jnp.int32)
    tile_count = draw_tile_count(jax.random.fold_in(streams_of[7], 71), 0)
    scale_table = jnp.clip(jnp.exp(jax.random.uniform(streams_of[6], (NSCALE,), jnp.float32, math.log(0.1), math.log(1.5))), 0.1, 1.5)
    return dict(vectors=vectors, tile_values=tile_values, tile_rows=tile_rows, tile_cols=tile_cols, tile_scale=tile_scale, tile_count=tile_count, scale_table=scale_table)


def block_weights(row_ids, col_ids, scale_ids, live_count, scale_table, row_index, col_index, piece_blocks, col_total):
    global_row = row_index * col_total * piece_blocks + row_ids
    global_col = ((col_ids // piece_blocks) * col_total + col_index) * piece_blocks + col_ids % piece_blocks
    looked = jnp.take(scale_table, scale_ids)
    halved = jnp.where(global_row == global_col, 0.5, 1.0) * looked
    is_live = jnp.arange(row_ids.shape[0], dtype=jnp.int32) < live_count
    return jnp.where(is_live, halved, 0.0).astype(jnp.float32)


def tile_sums(row_vec, col_vec, values, row_ids, col_ids, weight_of, row_start, col_start):
    matrices = values.reshape(-1, TILE, TILE).astype(jnp.float32)
    near = jnp.take(row_vec, row_ids, axis=1).astype(jnp.float32)
    distant = jnp.take(col_vec, col_ids, axis=1).astype(jnp.float32)
    forward = jnp.einsum("tij,ktj->kti", matrices, distant) * weight_of[None, :, None]
    mirrored = jnp.einsum("tij,kti->ktj", matrices, near) * weight_of[None, :, None]
    return row_start.at[:, row_ids].add(forward), col_start.at[:, col_ids].add(mirrored)


def reference(vectors, tile_values, tile_rows, tile_cols, tile_scale, tile_count, scale_table):
    piece_blocks = V // TILE
    row_blocks = N_COL * piece_blocks
    col_blocks = N_ROW * piece_blocks
    device_total = N_ROW * N_COL
    grid = vectors.reshape(NVEC, N_ROW, N_COL, V)

    def per_device(items):
        device, values, row_ids, col_ids, scale_ids, live_count = items
        row_index = device // N_COL
        col_index = device % N_COL
        row_vec = lax.dynamic_index_in_dim(grid, row_index, 1, keepdims=False).reshape(NVEC, row_blocks, TILE)
        col_vec = lax.dynamic_index_in_dim(grid, col_index, 2, keepdims=False).reshape(NVEC, col_blocks, TILE)
        weight_of = block_weights(row_ids, col_ids, scale_ids, live_count, scale_table, row_index, col_index, piece_blocks, N_COL)
        row_start = jnp.zeros((NVEC, row_blocks, TILE), jnp.float32)
        col_start = jnp.zeros((NVEC, col_blocks, TILE), jnp.float32)
        return tile_sums(row_vec, col_vec, values, row_ids, col_ids, weight_of, row_start, col_start)

    devices = jnp.arange(device_total, dtype=jnp.int32)
    row_part, col_part = lax.map(per_device, (
        devices,
        tile_values.reshape(device_total, TILES_DEV, TILE * TILE),
        tile_rows.reshape(device_total, TILES_DEV),
        tile_cols.reshape(device_total, TILES_DEV),
        tile_scale.reshape(device_total, TILES_DEV),
        tile_count.reshape(device_total)))
    row_total = row_part.reshape(N_ROW, N_COL, NVEC, N_COL * V).sum(axis=1)
    row_total = jnp.transpose(row_total, (1, 0, 2)).reshape(NVEC, N_ROW * N_COL * V)
    col_total = col_part.reshape(N_ROW, N_COL, NVEC, N_ROW, V).sum(axis=0)
    col_total = jnp.transpose(col_total, (1, 2, 0, 3)).reshape(NVEC, N_ROW * N_COL * V)
    return row_total + col_total
```

```python
import functools

import jax
import jax.numpy as jnp
from jax import lax
from jax.experimental import pallas as pl
from jax.experimental.pallas import tpu as pltpu
from jax.sharding import PartitionSpec as P

TILE = 64
NVEC = 4
LANES = 128
GROUP = 4
MESH = pl.DeviceIdType.MESH


def kernel(
    n_row, n_col, slots, piece_len,
    x_hbm, w_hbm, rows_hbm, cols_hbm, scale_hbm, count_hbm, table_hbm,
    out_ref,
    col_x, row_x, w_vm, rows_sm, cols_sm, scale_sm, count_sm, table_sm,
    rid_vm, cid_vm, wt_vm, row_send, row_recv, col_send, col_recv,
    local_sem, x_row_send, x_row_recv, x_col_send, x_col_recv,
    p_row_send, p_row_recv, p_col_send, p_col_recv,
):
    me_row = lax.axis_index("row")
    me_col = lax.axis_index("col")
    blocks = piece_len // TILE
    chunk = piece_len * NVEC // LANES
    depth = slots * NVEC

    copies = [
        pltpu.make_async_copy(src, dst, local_sem.at[i])
        for i, (src, dst) in enumerate((
            (x_hbm, col_x.at[0]),
            (x_hbm, row_x.at[0]),
            (rows_hbm, rows_sm),
            (cols_hbm, cols_sm),
            (scale_hbm, scale_sm),
            (count_hbm, count_sm),
            (table_hbm, table_sm),
            (w_hbm, w_vm),
        ))
    ]
    for copy in copies:
        copy.start()

    def along_col(d):
        return (me_row, lax.rem(me_col + d, n_col))

    def along_row(d):
        return (lax.rem(me_row + d, n_row), me_col)

    barrier = pltpu.get_barrier_semaphore()
    for d in range(1, n_col):
        pl.semaphore_signal(barrier, inc=1, device_id=along_col(d), device_id_type=MESH)
    for d in range(1, n_row):
        pl.semaphore_signal(barrier, inc=1, device_id=along_row(d), device_id_type=MESH)
    copies[0].wait()
    copies[1].wait()
    pl.semaphore_wait(barrier, n_col + n_row - 2)

    gather_row = [
        pltpu.make_async_remote_copy(
            src_ref=row_x.at[0], dst_ref=row_x.at[d], send_sem=x_row_send.at[d],
            recv_sem=x_row_recv.at[d], device_id=along_col(d), device_id_type=MESH)
        for d in range(1, n_col)
    ]
    gather_col = [
        pltpu.make_async_remote_copy(
            src_ref=col_x.at[0], dst_ref=col_x.at[d], send_sem=x_col_send.at[d],
            recv_sem=x_col_recv.at[d], device_id=along_row(d), device_id_type=MESH)
        for d in range(1, n_row)
    ]
    for copy in gather_row + gather_col:
        copy.start()

    for copy in copies[2:7]:
        copy.wait()
    upper = lax.broadcasted_iota(jnp.int32, (8, LANES), 0) < NVEC
    for v in range(slots // 2):
        a, b = 2 * v, 2 * v + 1
        here = pl.ds(8 * v, 8)
        rid_vm[here, :] = jnp.where(upper, rows_sm[0, 0, a], rows_sm[0, 0, b])
        cid_vm[here, :] = jnp.where(upper, cols_sm[0, 0, a], cols_sm[0, 0, b])
        wt_vm[here, :] = jnp.where(
            upper, table_sm[scale_sm[0, 0, a]], table_sm[scale_sm[0, 0, b]])
    rid = rid_vm[...]
    cid = cid_vm[...]
    sub = lax.broadcasted_iota(jnp.int32, (depth, LANES), 0)
    lane = lax.broadcasted_iota(jnp.int32, (depth, LANES), 1)
    half = lax.div(lane, TILE)
    rid_piece, rid_block = lax.div(rid, blocks), lax.rem(rid, blocks)
    cid_piece, cid_block = lax.div(cid, blocks), lax.rem(cid, blocks)
    global_row = me_row * (n_col * blocks) + rid
    global_col = (cid_piece * n_col + me_col) * blocks + cid_block
    weight = jnp.where(global_row == global_col, 0.5, 1.0) * wt_vm[...]
    weight = jnp.where(lax.div(sub, NVEC) < count_sm[0, 0], weight, 0.0)

    def places(piece, block, me, total):
        back = lax.rem(me - piece + total, total)
        target = back * chunk + lax.div(block, 2) * NVEC + lax.rem(sub, NVEC)
        across = lax.broadcasted_iota(jnp.int32, (depth, total * chunk), 1)
        down = lax.broadcasted_iota(jnp.int32, (total * chunk, depth), 0)
        take = jnp.where(across == target[:, :1], 1.0, 0.0).astype(jnp.bfloat16)
        put = jnp.where(down == jnp.transpose(target)[:1, :], 1.0, 0.0).astype(jnp.bfloat16)
        return take, jnp.concatenate([put, put], axis=1), lax.rem(block, 2)

    take_row, put_row, odd_row = places(rid_piece, rid_block, me_col, n_col)
    take_col, put_col, odd_col = places(cid_piece, cid_block, me_row, n_row)
    row_weight = jnp.where(half == odd_row, weight, 0.0)
    col_weight = jnp.where(half == odd_col, weight, 0.0)

    def pick(take, pieces, odd):
        both = jnp.dot(take, pieces, preferred_element_type=jnp.float32)
        kept = jnp.where(half == odd, both, 0.0)
        return (kept + pltpu.roll(kept, TILE, 1)).astype(jnp.bfloat16)

    def place(put, values):
        high = values.astype(jnp.bfloat16)
        low = (values - high.astype(jnp.float32)).astype(jnp.bfloat16)
        return jnp.dot(
            put, jnp.concatenate([high, low], axis=0), preferred_element_type=jnp.float32)

    rows_of = GROUP * NVEC
    wide = GROUP * TILE
    g_row = lax.div(lax.broadcasted_iota(jnp.int32, (rows_of, wide), 0), NVEC)
    g_col = lax.div(lax.broadcasted_iota(jnp.int32, (rows_of, wide), 1), TILE)
    same = g_row == g_col
    copies[7].wait()

    for copy in gather_col:
        copy.wait_recv()
    distant = pick(take_col, col_x[...].reshape(n_row * chunk, LANES), odd_col)
    parts = []
    for g in range(slots // GROUP):
        tiles = w_vm[g * wide:(g + 1) * wide, :]
        prod = lax.dot_general(
            distant[g * rows_of:(g + 1) * rows_of, :TILE], tiles, (((1,), (1,)), ((), ())),
            preferred_element_type=jnp.float32)
        prod = jnp.where(same, prod, 0.0)
        total = prod[:, :LANES]
        for i in range(LANES, wide, LANES):
            total = total + prod[:, i:i + LANES]
        parts.append(total + pltpu.roll(total, TILE, 1))
    forward = jnp.concatenate(parts, axis=0) * row_weight
    row_send[...] = place(put_row, forward).reshape(n_col, chunk, LANES)
    scatter_row = [
        pltpu.make_async_remote_copy(
            src_ref=row_send.at[d], dst_ref=row_recv.at[d], send_sem=p_row_send.at[d],
            recv_sem=p_row_recv.at[d], device_id=along_col(n_col - d), device_id_type=MESH)
        for d in range(1, n_col)
    ]
    for copy in scatter_row:
        copy.start()

    for copy in gather_row:
        copy.wait_recv()
    near = pick(take_row, row_x[...].reshape(n_col * chunk, LANES), odd_row)
    parts = []
    for g in range(slots // GROUP):
        tiles = w_vm[g * wide:(g + 1) * wide, :]
        left = near[g * rows_of:(g + 1) * rows_of, :]
        left = jnp.concatenate([left] * (wide // LANES), axis=1)
        left = jnp.where(same, left, jnp.zeros_like(left))
        prod = jnp.dot(left, tiles, preferred_element_type=jnp.float32)
        parts.append(jnp.concatenate([prod, prod], axis=1))
    mirrored = jnp.concatenate(parts, axis=0) * col_weight
    col_send[...] = place(put_col, mirrored).reshape(n_row, chunk, LANES)
    scatter_col = [
        pltpu.make_async_remote_copy(
            src_ref=col_send.at[d], dst_ref=col_recv.at[d], send_sem=p_col_send.at[d],
            recv_sem=p_col_recv.at[d], device_id=along_row(n_row - d), device_id_type=MESH)
        for d in range(1, n_row)
    ]
    for copy in scatter_col:
        copy.start()

    total = row_send[0] + col_send[0]
    for copy in gather_row + gather_col:
        copy.wait_send()
    for d, copy in enumerate(scatter_row, 1):
        copy.wait_recv()
        total = total + row_recv[d]
    for d, copy in enumerate(scatter_col, 1):
        copy.wait_recv()
        total = total + col_recv[d]
    out_ref[...] = total
    for copy in scatter_row + scatter_col:
        copy.wait_send()


def per_device(vectors, tile_values, tile_rows, tile_cols, tile_scale, tile_count, scale_table):
    n_row = lax.axis_size("row")
    n_col = lax.axis_size("col")
    piece_len = vectors.shape[1]
    slots = tile_rows.shape[-1]
    groups = piece_len // LANES
    chunk = groups * NVEC
    depth = slots * NVEC
    x = vectors.reshape(NVEC, groups, LANES).transpose(1, 0, 2).reshape(chunk, LANES)
    w = tile_values.reshape(slots * TILE, TILE)
    dma = pltpu.SemaphoreType.DMA
    out = pl.pallas_call(
        functools.partial(kernel, n_row, n_col, slots, piece_len),
        out_shape=jax.ShapeDtypeStruct((chunk, LANES), jnp.float32),
        in_specs=[pl.BlockSpec(memory_space=pl.ANY)] * 7,
        out_specs=pl.BlockSpec(memory_space=pltpu.VMEM),
        scratch_shapes=[
            pltpu.VMEM((n_row, chunk, LANES), jnp.bfloat16),
            pltpu.VMEM((n_col, chunk, LANES), jnp.bfloat16),
            pltpu.VMEM((slots * TILE, TILE), jnp.bfloat16),
            pltpu.SMEM(tile_rows.shape, jnp.int32),
            pltpu.SMEM(tile_cols.shape, jnp.int32),
            pltpu.SMEM(tile_scale.shape, jnp.int32),
            pltpu.SMEM(tile_count.shape, jnp.int32),
            pltpu.SMEM(scale_table.shape, jnp.float32),
            pltpu.VMEM((depth, LANES), jnp.int32),
            pltpu.VMEM((depth, LANES), jnp.int32),
            pltpu.VMEM((depth, LANES), jnp.float32),
            pltpu.VMEM((n_col, chunk, LANES), jnp.float32),
            pltpu.VMEM((n_col, chunk, LANES), jnp.float32),
            pltpu.VMEM((n_row, chunk, LANES), jnp.float32),
            pltpu.VMEM((n_row, chunk, LANES), jnp.float32),
            dma((8,)),
            dma((n_col,)), dma((n_col,)), dma((n_row,)), dma((n_row,)),
            dma((n_col,)), dma((n_col,)), dma((n_row,)), dma((n_row,)),
        ],
        compiler_params=pltpu.CompilerParams(collective_id=0, has_side_effects=True),
        name="lanczos",
    )(x, w, tile_rows, tile_cols, tile_scale, tile_count, scale_table)
    return out.reshape(groups, NVEC, LANES).transpose(1, 0, 2).reshape(NVEC, piece_len)


def solution(mesh):
    return jax.shard_map(
        per_device,
        mesh=mesh,
        in_specs=(
            P(None, ("row", "col")),
            P("row", "col", None, None),
            P("row", "col", None),
            P("row", "col", None),
            P("row", "col", None),
            P("row", "col"),
            P(),
        ),
        out_specs=P(None, ("row", "col")),
        check_vma=False,
    )
```

```python
import functools

import jax
import jax.numpy as jnp
from jax import lax
from jax.experimental import pallas as pl
from jax.experimental.pallas import tpu as pltpu
from jax.sharding import PartitionSpec as P

TILE = 64
NVEC = 4
LANES = 128
GROUP = 4
MESH = pl.DeviceIdType.MESH


def relayout(slots, tv_vm, w32_vm, w_vm):
    pack = LANES // TILE
    step = max(1, 2 * LANES // (pack * slots))
    depth = pack * step * slots
    r = lax.broadcasted_iota(jnp.int32, (depth, depth), 0)
    c = lax.broadcasted_iota(jnp.int32, (depth, depth), 1)
    slot, i = lax.div(r, pack * step), lax.rem(r, pack * step)
    source = (lax.rem(i, pack) * step + lax.div(i, pack)) * slots + slot
    order = jnp.where(c == source, 1.0, 0.0).astype(jnp.bfloat16)
    low_half = lax.broadcasted_iota(jnp.int32, (slots, LANES), 1) < TILE
    total = TILE * TILE // LANES
    for first in range(0, total, step):
        low, high = [], []
        for g in range(first, first + step):
            part = tv_vm[:, g * LANES:(g + 1) * LANES].astype(jnp.float32)
            turned = pltpu.roll(part, TILE, 1)
            low.append(jnp.where(low_half, part, turned).astype(jnp.bfloat16))
            high.append(jnp.where(low_half, turned, part).astype(jnp.bfloat16))
        moved = jnp.dot(
            order, jnp.concatenate(low + high, axis=0), preferred_element_type=jnp.float32)
        w32_vm[:, first * pack:(first + step) * pack, :] = moved.reshape(
            slots, pack * step, LANES)
    w_vm[...] = w32_vm[...].reshape(slots * TILE, LANES).astype(jnp.bfloat16)


def kernel(
    n_row, n_col, slots, piece_len,
    x_hbm, w_hbm, rows_hbm, cols_hbm, scale_hbm, count_hbm, table_hbm,
    out_ref,
    col_x, row_x, tv_vm, w32_vm, w_vm, rows_sm, cols_sm, scale_sm, count_sm, table_sm,
    rid_vm, cid_vm, wt_vm, row_send, row_recv, col_send, col_recv,
    local_sem, x_row_send, x_row_recv, x_col_send, x_col_recv,
    p_row_send, p_row_recv, p_col_send, p_col_recv,
):
    me_row = lax.axis_index("row")
    me_col = lax.axis_index("col")
    blocks = piece_len // TILE
    chunk = piece_len * NVEC // LANES
    depth = slots * NVEC

    copies = [
        pltpu.make_async_copy(src, dst, local_sem.at[i])
        for i, (src, dst) in enumerate((
            (x_hbm, col_x.at[0]),
            (x_hbm, row_x.at[0]),
            (rows_hbm, rows_sm),
            (cols_hbm, cols_sm),
            (scale_hbm, scale_sm),
            (count_hbm, count_sm),
            (table_hbm, table_sm),
            (w_hbm, tv_vm),
        ))
    ]
    for copy in copies:
        copy.start()

    def along_col(d):
        return (me_row, lax.rem(me_col + d, n_col))

    def along_row(d):
        return (lax.rem(me_row + d, n_row), me_col)

    barrier = pltpu.get_barrier_semaphore()
    for d in range(1, n_col):
        pl.semaphore_signal(barrier, inc=1, device_id=along_col(d), device_id_type=MESH)
    for d in range(1, n_row):
        pl.semaphore_signal(barrier, inc=1, device_id=along_row(d), device_id_type=MESH)
    copies[0].wait()
    copies[1].wait()
    pl.semaphore_wait(barrier, n_col + n_row - 2)

    gather_row = [
        pltpu.make_async_remote_copy(
            src_ref=row_x.at[0], dst_ref=row_x.at[d], send_sem=x_row_send.at[d],
            recv_sem=x_row_recv.at[d], device_id=along_col(d), device_id_type=MESH)
        for d in range(1, n_col)
    ]
    gather_col = [
        pltpu.make_async_remote_copy(
            src_ref=col_x.at[0], dst_ref=col_x.at[d], send_sem=x_col_send.at[d],
            recv_sem=x_col_recv.at[d], device_id=along_row(d), device_id_type=MESH)
        for d in range(1, n_row)
    ]
    for copy in gather_row + gather_col:
        copy.start()

    copies[7].wait()
    relayout(slots, tv_vm, w32_vm, w_vm)
    for copy in copies[2:7]:
        copy.wait()
    upper = lax.broadcasted_iota(jnp.int32, (8, LANES), 0) < NVEC
    for v in range(slots // 2):
        a, b = 2 * v, 2 * v + 1
        here = pl.ds(8 * v, 8)
        rid_vm[here, :] = jnp.where(upper, rows_sm[0, 0, a], rows_sm[0, 0, b])
        cid_vm[here, :] = jnp.where(upper, cols_sm[0, 0, a], cols_sm[0, 0, b])
        wt_vm[here, :] = jnp.where(
            upper, table_sm[scale_sm[0, 0, a]], table_sm[scale_sm[0, 0, b]])
    rid = rid_vm[...]
    cid = cid_vm[...]
    sub = lax.broadcasted_iota(jnp.int32, (depth, LANES), 0)
    lane = lax.broadcasted_iota(jnp.int32, (depth, LANES), 1)
    half = lax.div(lane, TILE)
    rid_piece, rid_block = lax.div(rid, blocks), lax.rem(rid, blocks)
    cid_piece, cid_block = lax.div(cid, blocks), lax.rem(cid, blocks)
    global_row = me_row * (n_col * blocks) + rid
    global_col = (cid_piece * n_col + me_col) * blocks + cid_block
    weight = jnp.where(global_row == global_col, 0.5, 1.0) * wt_vm[...]
    weight = jnp.where(lax.div(sub, NVEC) < count_sm[0, 0], weight, 0.0)

    def places(piece, block, me, total):
        back = lax.rem(me - piece + total, total)
        target = back * chunk + lax.div(block, 2) * NVEC + lax.rem(sub, NVEC)
        across = lax.broadcasted_iota(jnp.int32, (depth, total * chunk), 1)
        down = lax.broadcasted_iota(jnp.int32, (total * chunk, depth), 0)
        take = jnp.where(across == target[:, :1], 1.0, 0.0).astype(jnp.bfloat16)
        put = jnp.where(down == jnp.transpose(target)[:1, :], 1.0, 0.0).astype(jnp.bfloat16)
        return take, jnp.concatenate([put, put], axis=1), lax.rem(block, 2)

    take_row, put_row, odd_row = places(rid_piece, rid_block, me_col, n_col)
    take_col, put_col, odd_col = places(cid_piece, cid_block, me_row, n_row)
    row_weight = jnp.where(half == odd_row, weight, 0.0)
    col_weight = jnp.where(half == odd_col, weight, 0.0)

    def pick(take, pieces, odd):
        both = jnp.dot(take, pieces, preferred_element_type=jnp.float32)
        kept = jnp.where(half == odd, both, 0.0)
        return (kept + pltpu.roll(kept, TILE, 1)).astype(jnp.bfloat16)

    def place(put, values):
        high = values.astype(jnp.bfloat16)
        low = (values - high.astype(jnp.float32)).astype(jnp.bfloat16)
        return jnp.dot(
            put, jnp.concatenate([high, low], axis=0), preferred_element_type=jnp.float32)

    rows_of = GROUP * NVEC
    wide = GROUP * TILE
    g_row = lax.div(lax.broadcasted_iota(jnp.int32, (rows_of, wide), 0), NVEC)
    g_col = lax.div(lax.broadcasted_iota(jnp.int32, (rows_of, wide), 1), TILE)
    same = g_row == g_col

    for copy in gather_col:
        copy.wait_recv()
    distant = pick(take_col, col_x[...].reshape(n_row * chunk, LANES), odd_col)
    parts = []
    for g in range(slots // GROUP):
        tiles = w_vm[g * wide:(g + 1) * wide, :]
        prod = lax.dot_general(
            distant[g * rows_of:(g + 1) * rows_of, :TILE], tiles[:, :TILE],
            (((1,), (1,)), ((), ())),
            preferred_element_type=jnp.float32)
        prod = jnp.where(same, prod, 0.0)
        total = prod[:, :LANES]
        for i in range(LANES, wide, LANES):
            total = total + prod[:, i:i + LANES]
        parts.append(total + pltpu.roll(total, TILE, 1))
    forward = jnp.concatenate(parts, axis=0) * row_weight
    row_send[...] = place(put_row, forward).reshape(n_col, chunk, LANES)
    scatter_row = [
        pltpu.make_async_remote_copy(
            src_ref=row_send.at[d], dst_ref=row_recv.at[d], send_sem=p_row_send.at[d],
            recv_sem=p_row_recv.at[d], device_id=along_col(n_col - d), device_id_type=MESH)
        for d in range(1, n_col)
    ]
    for copy in scatter_row:
        copy.start()

    for copy in gather_row:
        copy.wait_recv()
    near = pick(take_row, row_x[...].reshape(n_col * chunk, LANES), odd_row)
    parts = []
    for g in range(slots // GROUP):
        tiles = w_vm[g * wide:(g + 1) * wide, :]
        left = near[g * rows_of:(g + 1) * rows_of, :]
        left = jnp.concatenate([left] * (wide // LANES), axis=1)
        left = jnp.where(same, left, jnp.zeros_like(left))
        parts.append(jnp.dot(left, tiles, preferred_element_type=jnp.float32))
    mirrored = jnp.concatenate(parts, axis=0) * col_weight
    col_send[...] = place(put_col, mirrored).reshape(n_row, chunk, LANES)
    scatter_col = [
        pltpu.make_async_remote_copy(
            src_ref=col_send.at[d], dst_ref=col_recv.at[d], send_sem=p_col_send.at[d],
            recv_sem=p_col_recv.at[d], device_id=along_row(n_row - d), device_id_type=MESH)
        for d in range(1, n_row)
    ]
    for copy in scatter_col:
        copy.start()

    total = row_send[0] + col_send[0]
    for copy in gather_row + gather_col:
        copy.wait_send()
    for d, copy in enumerate(scatter_row, 1):
        copy.wait_recv()
        total = total + row_recv[d]
    for d, copy in enumerate(scatter_col, 1):
        copy.wait_recv()
        total = total + col_recv[d]
    out_ref[...] = total
    for copy in scatter_row + scatter_col:
        copy.wait_send()


def per_device(vectors, tile_values, tile_rows, tile_cols, tile_scale, tile_count, scale_table):
    n_row = lax.axis_size("row")
    n_col = lax.axis_size("col")
    piece_len = vectors.shape[1]
    slots = tile_rows.shape[-1]
    groups = piece_len // LANES
    chunk = groups * NVEC
    depth = slots * NVEC
    x = vectors.reshape(NVEC, groups, LANES).transpose(1, 0, 2).reshape(chunk, LANES)
    w = tile_values.reshape(slots, TILE * TILE)
    dma = pltpu.SemaphoreType.DMA
    out = pl.pallas_call(
        functools.partial(kernel, n_row, n_col, slots, piece_len),
        out_shape=jax.ShapeDtypeStruct((chunk, LANES), jnp.float32),
        in_specs=[pl.BlockSpec(memory_space=pltpu.HBM)] * 7,
        out_specs=pl.BlockSpec(memory_space=pltpu.VMEM),
        scratch_shapes=[
            pltpu.VMEM((n_row, chunk, LANES), jnp.bfloat16),
            pltpu.VMEM((n_col, chunk, LANES), jnp.bfloat16),
            pltpu.VMEM((slots, TILE * TILE), jnp.bfloat16),
            pltpu.VMEM((slots, TILE, LANES), jnp.float32),
            pltpu.VMEM((slots * TILE, LANES), jnp.bfloat16),
            pltpu.SMEM(tile_rows.shape, jnp.int32),
            pltpu.SMEM(tile_cols.shape, jnp.int32),
            pltpu.SMEM(tile_scale.shape, jnp.int32),
            pltpu.SMEM(tile_count.shape, jnp.int32),
            pltpu.SMEM(scale_table.shape, jnp.float32),
            pltpu.VMEM((depth, LANES), jnp.int32),
            pltpu.VMEM((depth, LANES), jnp.int32),
            pltpu.VMEM((depth, LANES), jnp.float32),
            pltpu.VMEM((n_col, chunk, LANES), jnp.float32),
            pltpu.VMEM((n_col, chunk, LANES), jnp.float32),
            pltpu.VMEM((n_row, chunk, LANES), jnp.float32),
            pltpu.VMEM((n_row, chunk, LANES), jnp.float32),
            dma((8,)),
            dma((n_col,)), dma((n_col,)), dma((n_row,)), dma((n_row,)),
            dma((n_col,)), dma((n_col,)), dma((n_row,)), dma((n_row,)),
        ],
        compiler_params=pltpu.CompilerParams(collective_id=0, has_side_effects=True, vmem_limit_bytes=24 * 1024 * 1024),
        name="lanczos",
    )(x, w, tile_rows, tile_cols, tile_scale, tile_count, scale_table)
    return out.reshape(groups, NVEC, LANES).transpose(1, 0, 2).reshape(NVEC, piece_len)


def solution(mesh):
    return jax.shard_map(
        per_device,
        mesh=mesh,
        in_specs=(
            P(None, ("row", "col")),
            P("row", "col", None, None),
            P("row", "col", None),
            P("row", "col", None),
            P("row", "col", None),
            P("row", "col"),
            P(),
        ),
        out_specs=P(None, ("row", "col")),
        check_vma=False,
    )
```

```python
import functools

import jax
import jax.numpy as jnp
from jax import lax
from jax.experimental import pallas as pl
from jax.experimental.pallas import tpu as pltpu
from jax.sharding import PartitionSpec as P

TILE = 64
NVEC = 4
LANES = 128
GROUP = 4
MESH = pl.DeviceIdType.MESH


def relayout(slots, tv_vm, w32_vm, w_vm):
    pack = LANES // TILE
    step = max(1, 2 * LANES // (pack * slots))
    depth = pack * step * slots
    r = lax.broadcasted_iota(jnp.int32, (depth, depth), 0)
    c = lax.broadcasted_iota(jnp.int32, (depth, depth), 1)
    slot, i = lax.div(r, pack * step), lax.rem(r, pack * step)
    source = (lax.rem(i, pack) * step + lax.div(i, pack)) * slots + slot
    order = jnp.where(c == source, 1.0, 0.0).astype(jnp.bfloat16)
    low_half = lax.broadcasted_iota(jnp.int32, (slots, LANES), 1) < TILE
    total = TILE * TILE // LANES
    for first in range(0, total, step):
        low, high = [], []
        for g in range(first, first + step):
            part = tv_vm[:, g * LANES:(g + 1) * LANES].astype(jnp.float32)
            turned = pltpu.roll(part, TILE, 1)
            low.append(jnp.where(low_half, part, turned).astype(jnp.bfloat16))
            high.append(jnp.where(low_half, turned, part).astype(jnp.bfloat16))
        moved = jnp.dot(
            order, jnp.concatenate(low + high, axis=0), preferred_element_type=jnp.float32)
        w32_vm[:, first * pack:(first + step) * pack, :] = moved.reshape(
            slots, pack * step, LANES)
    w_vm[...] = w32_vm[...].reshape(slots * TILE, LANES).astype(jnp.bfloat16)


def kernel(
    n_row, n_col, slots, piece_len,
    x_hbm, w_hbm, rows_hbm, cols_hbm, scale_hbm, count_hbm, table_hbm,
    out_ref,
    col_x, row_x, tv_vm, w32_vm, w_vm, rows_sm, cols_sm, scale_sm, count_sm, table_sm,
    rid_vm, cid_vm, wt_vm, row_send, row_recv, col_send, col_recv,
    local_sem, x_row_send, x_row_recv, x_col_send, x_col_recv,
    p_row_send, p_row_recv, p_col_send, p_col_recv,
):
    me_row = lax.axis_index("row")
    me_col = lax.axis_index("col")
    blocks = piece_len // TILE
    chunk = piece_len * NVEC // LANES
    depth = slots * NVEC

    copies = [
        pltpu.make_async_copy(src, dst, local_sem.at[i])
        for i, (src, dst) in enumerate((
            (x_hbm, col_x.at[0]),
            (x_hbm, row_x.at[0]),
            (rows_hbm, rows_sm),
            (cols_hbm, cols_sm),
            (scale_hbm, scale_sm),
            (count_hbm, count_sm),
            (table_hbm, table_sm),
            (w_hbm, tv_vm),
        ))
    ]
    for copy in copies:
        copy.start()

    def along_col(d):
        return (me_row, lax.rem(me_col + d, n_col))

    def along_row(d):
        return (lax.rem(me_row + d, n_row), me_col)

    barrier = pltpu.get_barrier_semaphore()
    for d in range(1, n_col):
        pl.semaphore_signal(barrier, inc=1, device_id=along_col(d), device_id_type=MESH)
    for d in range(1, n_row):
        pl.semaphore_signal(barrier, inc=1, device_id=along_row(d), device_id_type=MESH)
    copies[0].wait()
    copies[1].wait()
    pl.semaphore_wait(barrier, n_col + n_row - 2)

    gather_row = [
        pltpu.make_async_remote_copy(
            src_ref=row_x.at[0], dst_ref=row_x.at[d], send_sem=x_row_send.at[d],
            recv_sem=x_row_recv.at[d], device_id=along_col(d), device_id_type=MESH)
        for d in range(1, n_col)
    ]
    gather_col = [
        pltpu.make_async_remote_copy(
            src_ref=col_x.at[0], dst_ref=col_x.at[d], send_sem=x_col_send.at[d],
            recv_sem=x_col_recv.at[d], device_id=along_row(d), device_id_type=MESH)
        for d in range(1, n_row)
    ]
    for copy in gather_row + gather_col:
        copy.start()

    copies[7].wait()
    relayout(slots, tv_vm, w32_vm, w_vm)
    for copy in copies[2:7]:
        copy.wait()
    upper = lax.broadcasted_iota(jnp.int32, (8, LANES), 0) < NVEC
    for v in range(slots // 2):
        a, b = 2 * v, 2 * v + 1
        here = pl.ds(8 * v, 8)
        rid_vm[here, :] = jnp.where(upper, rows_sm[0, 0, a], rows_sm[0, 0, b])
        cid_vm[here, :] = jnp.where(upper, cols_sm[0, 0, a], cols_sm[0, 0, b])
        wt_vm[here, :] = jnp.where(
            upper, table_sm[scale_sm[0, 0, a]], table_sm[scale_sm[0, 0, b]])
    rid = rid_vm[...]
    cid = cid_vm[...]
    sub = lax.broadcasted_iota(jnp.int32, (depth, LANES), 0)
    lane = lax.broadcasted_iota(jnp.int32, (depth, LANES), 1)
    half = lax.div(lane, TILE)
    rid_piece, rid_block = lax.div(rid, blocks), lax.rem(rid, blocks)
    cid_piece, cid_block = lax.div(cid, blocks), lax.rem(cid, blocks)
    global_row = me_row * (n_col * blocks) + rid
    global_col = (cid_piece * n_col + me_col) * blocks + cid_block
    weight = jnp.where(global_row == global_col, 0.5, 1.0) * wt_vm[...]
    weight = jnp.where(lax.div(sub, NVEC) < count_sm[0, 0], weight, 0.0)

    def places(piece, block, me, total):
        back = lax.rem(me - piece + total, total)
        target = back * chunk + lax.div(block, 2) * NVEC + lax.rem(sub, NVEC)
        across = lax.broadcasted_iota(jnp.int32, (depth, total * chunk), 1)
        down = lax.broadcasted_iota(jnp.int32, (total * chunk, depth), 0)
        take = jnp.where(across == target[:, :1], 1.0, 0.0).astype(jnp.bfloat16)
        put = jnp.where(down == jnp.transpose(target)[:1, :], 1.0, 0.0).astype(jnp.bfloat16)
        return take, jnp.concatenate([put, put], axis=1), lax.rem(block, 2)

    take_row, put_row, odd_row = places(rid_piece, rid_block, me_col, n_col)
    take_col, put_col, odd_col = places(cid_piece, cid_block, me_row, n_row)
    row_weight = jnp.where(half == odd_row, weight, 0.0)
    col_weight = jnp.where(half == odd_col, weight, 0.0)

    def pick(take, pieces, odd):
        both = jnp.dot(take, pieces, preferred_element_type=jnp.float32)
        kept = jnp.where(half == odd, both, 0.0)
        return (kept + pltpu.roll(kept, TILE, 1)).astype(jnp.bfloat16)

    def place(put, values):
        high = values.astype(jnp.bfloat16)
        low = (values - high.astype(jnp.float32)).astype(jnp.bfloat16)
        return jnp.dot(
            put, jnp.concatenate([high, low], axis=0), preferred_element_type=jnp.float32)

    rows_of = GROUP * NVEC
    wide = GROUP * TILE
    g_row = lax.div(lax.broadcasted_iota(jnp.int32, (rows_of, wide), 0), NVEC)
    g_col = lax.div(lax.broadcasted_iota(jnp.int32, (rows_of, wide), 1), TILE)
    same = g_row == g_col

    for copy in gather_col:
        copy.wait_recv()
    distant = pick(take_col, col_x[...].reshape(n_row * chunk, LANES), odd_col)
    parts = []
    for g in range(slots // GROUP):
        tiles = w_vm[g * wide:(g + 1) * wide, :]
        prod = lax.dot_general(
            distant[g * rows_of:(g + 1) * rows_of, :TILE], tiles[:, :TILE],
            (((1,), (1,)), ((), ())),
            preferred_element_type=jnp.float32)
        prod = jnp.where(same, prod, 0.0)
        total = prod[:, :LANES]
        for i in range(LANES, wide, LANES):
            total = total + prod[:, i:i + LANES]
        parts.append(total + pltpu.roll(total, TILE, 1))
    forward = jnp.concatenate(parts, axis=0) * row_weight
    row_send[...] = place(put_row, forward).reshape(n_col, chunk, LANES)
    scatter_row = [
        pltpu.make_async_remote_copy(
            src_ref=row_send.at[d], dst_ref=row_recv.at[d], send_sem=p_row_send.at[d],
            recv_sem=p_row_recv.at[d], device_id=along_col(n_col - d), device_id_type=MESH)
        for d in range(1, n_col)
    ]
    for copy in scatter_row:
        copy.start()

    for copy in gather_row:
        copy.wait_recv()
    near = pick(take_row, row_x[...].reshape(n_col * chunk, LANES), odd_row)
    parts = []
    for g in range(slots // GROUP):
        tiles = w_vm[g * wide:(g + 1) * wide, :]
        left = near[g * rows_of:(g + 1) * rows_of, :]
        left = jnp.concatenate([left] * (wide // LANES), axis=1)
        left = jnp.where(same, left, jnp.zeros_like(left))
        parts.append(jnp.dot(left, tiles, preferred_element_type=jnp.float32))
    mirrored = jnp.concatenate(parts, axis=0) * col_weight
    col_send[...] = place(put_col, mirrored).reshape(n_row, chunk, LANES)
    scatter_col = [
        pltpu.make_async_remote_copy(
            src_ref=col_send.at[d], dst_ref=col_recv.at[d], send_sem=p_col_send.at[d],
            recv_sem=p_col_recv.at[d], device_id=along_row(n_row - d), device_id_type=MESH)
        for d in range(1, n_row)
    ]
    for copy in scatter_col:
        copy.start()

    total = row_send[0] + col_send[0]
    for copy in gather_row + gather_col:
        copy.wait_send()
    for d, copy in enumerate(scatter_row, 1):
        copy.wait_recv()
        total = total + row_recv[d]
    for d, copy in enumerate(scatter_col, 1):
        copy.wait_recv()
        total = total + col_recv[d]
    out_ref[...] = total
    for copy in scatter_row + scatter_col:
        copy.wait_send()


def per_device(vectors, tile_values, tile_rows, tile_cols, tile_scale, tile_count, scale_table):
    n_row = lax.axis_size("row")
    n_col = lax.axis_size("col")
    piece_len = vectors.shape[1]
    slots = tile_rows.shape[-1]
    groups = piece_len // LANES
    chunk = groups * NVEC
    depth = slots * NVEC
    x = vectors.reshape(NVEC, groups, LANES).transpose(1, 0, 2).reshape(chunk, LANES)
    w = tile_values.reshape(slots, TILE * TILE)
    dma = pltpu.SemaphoreType.DMA
    out = pl.pallas_call(
        functools.partial(kernel, n_row, n_col, slots, piece_len),
        out_shape=pltpu.VMEM((chunk, LANES), jnp.float32),
        in_specs=[pl.BlockSpec(memory_space=pltpu.HBM)] * 7,
        out_specs=pl.BlockSpec(memory_space=pltpu.VMEM),
        scratch_shapes=[
            pltpu.VMEM((n_row, chunk, LANES), jnp.bfloat16),
            pltpu.VMEM((n_col, chunk, LANES), jnp.bfloat16),
            pltpu.VMEM((slots, TILE * TILE), jnp.bfloat16),
            pltpu.VMEM((slots, TILE, LANES), jnp.float32),
            pltpu.VMEM((slots * TILE, LANES), jnp.bfloat16),
            pltpu.SMEM(tile_rows.shape, jnp.int32),
            pltpu.SMEM(tile_cols.shape, jnp.int32),
            pltpu.SMEM(tile_scale.shape, jnp.int32),
            pltpu.SMEM(tile_count.shape, jnp.int32),
            pltpu.SMEM(scale_table.shape, jnp.float32),
            pltpu.VMEM((depth, LANES), jnp.int32),
            pltpu.VMEM((depth, LANES), jnp.int32),
            pltpu.VMEM((depth, LANES), jnp.float32),
            pltpu.VMEM((n_col, chunk, LANES), jnp.float32),
            pltpu.VMEM((n_col, chunk, LANES), jnp.float32),
            pltpu.VMEM((n_row, chunk, LANES), jnp.float32),
            pltpu.VMEM((n_row, chunk, LANES), jnp.float32),
            dma((8,)),
            dma((n_col,)), dma((n_col,)), dma((n_row,)), dma((n_row,)),
            dma((n_col,)), dma((n_col,)), dma((n_row,)), dma((n_row,)),
        ],
        compiler_params=pltpu.CompilerParams(collective_id=0, has_side_effects=True),
        name="lanczos",
    )(x, w, tile_rows, tile_cols, tile_scale, tile_count, scale_table)
    return out.reshape(groups, NVEC, LANES).transpose(1, 0, 2).reshape(NVEC, piece_len)


def solution(mesh):
    return jax.shard_map(
        per_device,
        mesh=mesh,
        in_specs=(
            P(None, ("row", "col")),
            P("row", "col", None, None),
            P("row", "col", None),
            P("row", "col", None),
            P("row", "col", None),
            P("row", "col"),
            P(),
        ),
        out_specs=P(None, ("row", "col")),
        check_vma=False,
    )
```
